32 devices in a mesh: dom: 8 (over z, y), batch: 4 (over x, core).
Axes of the slice: x: 2, y: 2, z: 4, core: 2. Of those that a mesh axis runs over, the one named last changes fastest.
Arguments:
- signal: bfloat16 [4096, 4, 4, 256], P('dom', 'batch'), may hold values from -6 to 6
- cotangent: bfloat16 [4096, 4, 3, 256], P('dom', 'batch'), may hold values from -6 to 6
- conv_weight: bfloat16 [2, 2, 256, 256], replicated, may hold values from -0.25 to 0.25
- mix_weight: bfloat16 [3, 256, 256], replicated, may hold values from -0.21875 to 0.21875
- send_rows: int32 [64, 16], P('dom'), may hold values from 0 to 511
- send_mask: int32 [64, 16], P('dom'), may hold values 0 or 1
- tile_vals: bfloat16 [128, 128, 128], P('dom'), may hold values from -0.26953125 to 0.26953125
- tile_row: int32 [128], P('dom'), may hold values from 0 to 3
- tile_col: int32 [128], P('dom'), may hold values from 0 to 5
- tile_mask: int32 [128], P('dom'), may hold values 0 or 1
- hub_owner: int32 [8], replicated, may hold values from 0 to 7, as said below
- hub_rows: int32 [8, 16], replicated, may hold values from 0 to 511
Outputs:
- layer_out: bfloat16 [4096, 4, 3, 256], P('dom', 'batch')
- signal_grad: bfloat16 [4096, 4, 4, 256], P('dom', 'batch')
- conv_grad: float32 [2, 2, 256, 256], replicated
- mix_grad: float32 [3, 256, 256], replicated
The draws below stay inside these ranges and needn't reach their ends.
Inputs may be any that keep to these rules, and one draw needn't show every extreme that they name: `hub_owner`: each owner slot names a different partition.
All inputs are finite; a program needn't handle non-finite values. No bound on the sum of `send_mask` or of `tile_mask` on one device may be relied on, other than what follows from the above.
Results may differ from the reference program's by a relative error of at most 0.0056.
Values may be sent and summed in bfloat16 or wider, within the bound.
A program may use at most 128 MiB of HBM per device.

```python
import math
import jax
import jax.numpy as jnp
from jax import lax

C = 256
HIST = 4
NODE_DEV = 512
BLK = 128
OWNERS = 8
HUB_PER = 16
T1 = 3
TILES = 16
CAP = 16
HALO = 128
EXT = 768
NODES = 4096
BATCH = 4
N_DOM = 8


def draw_hub_owner(key, part):
    inner_key = jax.random.fold_in(key, 11)
    order_key = jax.random.fold_in(key, 23)
    middle = jax.random.permutation(inner_key, N_DOM - 2)[:OWNERS - 2].astype(jnp.int32) + 1
    ends = jnp.array([0, N_DOM - 1], dtype=jnp.int32)
    owners = jnp.concatenate([ends, middle], 0)
    order = jax.random.permutation(order_key, OWNERS)
    return owners[order].astype(jnp.int32)


def set_ends(drawn, rng, low, high):
    longest = drawn.shape.index(max(drawn.shape))
    spots = []
    for shift in (0, 1):
        where = [jax.random.randint(jax.random.fold_in(rng, axis), (), 0, length) for axis, length in enumerate(drawn.shape)]
        where[longest] = (where[longest] + shift) % drawn.shape[longest]
        spots.append(tuple(where))
    return drawn.at[spots[0]].set(low).at[spots[1]].set(high)


def levels(key, dims, split, smallest, largest):
    factor_of = 1.0
    for position, parts in split:
        draws = jax.random.uniform(jax.random.fold_in(jax.random.fold_in(key, 6), position), (parts,), jnp.float32, smallest / len(split), largest / len(split))
        factor_of = factor_of * jnp.repeat(jnp.exp(draws), dims[position] // parts).reshape((-1,) + (1,) * (len(dims) - 1 - position))
    return factor_of


def gaussian(stream_key, dims, deviation, bound, pieces=(), held_as=jnp.bfloat16):
    values = jax.random.normal(stream_key, dims, jnp.float32) * deviation
    if len(pieces) > 0:
        values = levels(stream_key, dims, pieces, -0.22, 0.18) * values
    return jnp.clip(values, min=-bound, max=bound).astype(held_as)


def setup_inputs(seed: int = 0) -> dict:
    splits = jax.random.split(jax.random.key(seed), 13)
    signal = gaussian(splits[0], (NODES, BATCH, HIST, C), 1.0, 6.0, ((0, 8), (1, 4)))
    cotangent = gaussian(splits[1], (NODES, BATCH, T1, C), 1.0, 6.0, ((0, 8), (1, 4)))
    conv_weight = gaussian(splits[2], (2, 2, C, C), (2 * C) ** -0.5, 0.25)
    mix_weight = gaussian(splits[3], (3, C, C), (3 * C) ** -0.5, 0.21875)
    send_rows = set_ends(jax.random.randint(splits[4], (N_DOM * N_DOM, CAP), 0, NODE_DEV), jax.random.fold_in(splits[4], 1), 0, NODE_DEV - 1).astype(jnp.int32)
    send_mask = set_ends((jax.random.randint(splits[5], (N_DOM * N_DOM, CAP), 0, 3) < 2).astype(jnp.int32), jax.random.fold_in(splits[5], 1), 0, 1)
    tile_vals = gaussian(splits[6], (N_DOM * TILES, BLK, BLK), 0.045, 0.26953125, ((0, 8),))
    tile_row = set_ends(jax.random.randint(splits[7], (N_DOM * TILES,), 0, NODE_DEV // BLK), jax.random.fold_in(splits[7], 1), 0, (NODE_DEV // BLK) - 1).astype(jnp.int32)
    tile_col = set_ends(jax.random.randint(splits[8], (N_DOM * TILES,), 0, EXT // BLK), jax.random.fold_in(splits[8], 1), 0, (EXT // BLK) - 1).astype(jnp.int32)
    tile_mask = set_ends((jax.random.randint(splits[9], (N_DOM * TILES,), 0, 4) < 3).astype(jnp.int32), jax.random.fold_in(splits[9], 1), 0, 1)
    hub_owner = draw_hub_owner(jax.random.fold_in(splits[12], 71), 0)
    hub_rows = set_ends(jax.random.randint(splits[11], (OWNERS, HUB_PER), 0, NODE_DEV), jax.random.fold_in(splits[11], 1), 0, NODE_DEV - 1).astype(jnp.int32)
    return dict(signal=signal, cotangent=cotangent, conv_weight=conv_weight, mix_weight=mix_weight, send_rows=send_rows, send_mask=send_mask, tile_vals=tile_vals, tile_row=tile_row, tile_col=tile_col, tile_mask=tile_mask, hub_owner=hub_owner, hub_rows=hub_rows)


highest = lax.Precision.HIGHEST

def tile_apply(ext_rows, tile_block, row_ids, col_ids, tile_keep, row_tiles):
    block_rows = tile_block.shape[1]
    features = ext_rows.shape[1]
    chosen = ext_rows.reshape(-1, block_rows, features)[col_ids]
    product = jnp.einsum('tij,tjf->tif', tile_block.astype(jnp.float32), chosen.astype(jnp.float32), precision=highest)
    product = product * tile_keep.astype(jnp.float32)[:, None, None]
    onehot = (row_ids[None, :] == jnp.arange(row_tiles, dtype=jnp.int32)[:, None]).astype(jnp.float32)
    return jnp.einsum('rt,tif->rif', onehot, product, precision=highest).reshape(row_tiles * block_rows, features)

def tile_back(own_rows, tile_block, row_ids, col_ids, tile_keep, col_tiles):
    block_rows = tile_block.shape[1]
    features = own_rows.shape[1]
    chosen = own_rows.reshape(-1, block_rows, features)[row_ids]
    product = jnp.einsum('tji,tjf->tif', tile_block.astype(jnp.float32), chosen.astype(jnp.float32), precision=highest)
    product = product * tile_keep.astype(jnp.float32)[:, None, None]
    onehot = (col_ids[None, :] == jnp.arange(col_tiles, dtype=jnp.int32)[:, None]).astype(jnp.float32)
    return jnp.einsum('ct,tif->cif', onehot, product, precision=highest).reshape(col_tiles * block_rows, features)

def device_graph(graph, device):
    send_rows, send_mask, tile_vals, tile_row, tile_col, tile_mask, hub_owner, hub_rows = graph
    sources = lax.dynamic_index_in_dim(send_rows.reshape(N_DOM, N_DOM, CAP), device, 1, keepdims=False)
    source_keep = lax.dynamic_index_in_dim(send_mask.reshape(N_DOM, N_DOM, CAP), device, 1, keepdims=False)
    halo_index = (jnp.arange(N_DOM, dtype=jnp.int32)[:, None] * NODE_DEV + sources).reshape(-1).astype(jnp.int32)
    start = (device * TILES).astype(jnp.int32)
    tiles = (lax.dynamic_slice_in_dim(tile_vals, start, TILES, 0), lax.dynamic_slice_in_dim(tile_row, start, TILES, 0), lax.dynamic_slice_in_dim(tile_col, start, TILES, 0), lax.dynamic_slice_in_dim(tile_mask, start, TILES, 0))
    return (halo_index, source_keep.reshape(-1), tiles)

def hub_index_of(graph):
    hub_owner, hub_rows = (graph[6], graph[7])
    return (hub_owner[:, None] * NODE_DEV + hub_rows).reshape(-1).astype(jnp.int32)

def spread(field, graph):
    hub_index = hub_index_of(graph)
    hubs = field[hub_index]

    def per_device(device):
        halo_index, halo_keep, tiles = device_graph(graph, device)
        own = lax.dynamic_slice_in_dim(field, (device * NODE_DEV).astype(jnp.int32), NODE_DEV, 0)
        halo = field[halo_index] * halo_keep.astype(field.dtype)[:, None]
        ext_rows = jnp.concatenate([own, halo, hubs], 0)
        return tile_apply(ext_rows, tiles[0], tiles[1], tiles[2], tiles[3], NODE_DEV // BLK)
    return lax.map(per_device, jnp.arange(N_DOM, dtype=jnp.int32)).reshape(NODES, -1)

def gather_back(field, graph):
    hub_index = hub_index_of(graph)

    def per_device(carry, device):
        halo_index, halo_keep, tiles = device_graph(graph, device)
        start = (device * NODE_DEV).astype(jnp.int32)
        own = lax.dynamic_slice_in_dim(field, start, NODE_DEV, 0)
        ext_grad = tile_back(own, tiles[0], tiles[1], tiles[2], tiles[3], EXT // BLK)
        block = lax.dynamic_slice_in_dim(carry, start, NODE_DEV, 0) + ext_grad[:NODE_DEV]
        carry = lax.dynamic_update_slice_in_dim(carry, block, start, 0)
        carry = carry.at[halo_index].add(ext_grad[NODE_DEV:NODE_DEV + HALO] * halo_keep.astype(jnp.float32)[:, None])
        carry = carry.at[hub_index].add(ext_grad[NODE_DEV + HALO:])
        return (carry, None)
    total, unused = lax.scan(per_device, jnp.zeros(field.shape, jnp.float32), jnp.arange(N_DOM, dtype=jnp.int32))
    return total

def mm(left, right):
    return jnp.dot(left, right, preferred_element_type=jnp.float32)

def one_sample(signal_s, grad_s, conv_weight, mix_weight, graph):
    earlier = signal_s[:, :-1, :].reshape(-1, C)
    later = signal_s[:, 1:, :].reshape(-1, C)
    filt = mm(earlier, conv_weight[0, 0]) + mm(later, conv_weight[0, 1])
    gate = mm(earlier, conv_weight[1, 0]) + mm(later, conv_weight[1, 1])
    tanh_filt = jnp.tanh(filt)
    sig_gate = jax.nn.sigmoid(gate)
    hidden = (tanh_filt * sig_gate).astype(jnp.bfloat16)
    hop_one = spread(hidden.reshape(NODES, T1 * C), graph).astype(jnp.bfloat16).reshape(-1, C)
    hop_two = spread(hop_one.reshape(NODES, T1 * C), graph).astype(jnp.bfloat16).reshape(-1, C)
    mixed = later.astype(jnp.float32) + mm(hidden, mix_weight[0]) + mm(hop_one, mix_weight[1]) + mm(hop_two, mix_weight[2])
    layer_out = mixed.astype(jnp.bfloat16).reshape(NODES, T1, C)
    grad_out = grad_s.reshape(-1, C)
    mix_part = jnp.stack([mm(hidden.T, grad_out), mm(hop_one.T, grad_out), mm(hop_two.T, grad_out)])
    back_two = mm(grad_out, mix_weight[2].T).astype(jnp.bfloat16)
    back_one = mm(grad_out, mix_weight[1].T) + gather_back(back_two.reshape(NODES, T1 * C), graph).reshape(-1, C)
    back_one = back_one.astype(jnp.bfloat16)
    grad_hidden = mm(grad_out, mix_weight[0].T) + gather_back(back_one.reshape(NODES, T1 * C), graph).reshape(-1, C)
    grad_filt = (grad_hidden * sig_gate * (1.0 - tanh_filt * tanh_filt)).astype(jnp.bfloat16)
    grad_gate = (grad_hidden * tanh_filt * sig_gate * (1.0 - sig_gate)).astype(jnp.bfloat16)
    conv_part = jnp.stack([jnp.stack([mm(earlier.T, grad_filt), mm(later.T, grad_filt)]), jnp.stack([mm(earlier.T, grad_gate), mm(later.T, grad_gate)])])
    into_earlier = (mm(grad_filt, conv_weight[0, 0].T) + mm(grad_gate, conv_weight[1, 0].T)).reshape(NODES, T1, C)
    into_later = (mm(grad_filt, conv_weight[0, 1].T) + mm(grad_gate, conv_weight[1, 1].T) + grad_out.astype(jnp.float32)).reshape(NODES, T1, C)
    signal_grad = jnp.pad(into_earlier, ((0, 0), (0, 1), (0, 0))) + jnp.pad(into_later, ((0, 0), (1, 0), (0, 0)))
    return (layer_out, signal_grad.astype(jnp.bfloat16), conv_part, mix_part)

def reference(signal, cotangent, conv_weight, mix_weight, send_rows, send_mask, tile_vals, tile_row, tile_col, tile_mask, hub_owner, hub_rows):
    graph = (send_rows, send_mask, tile_vals, tile_row, tile_col, tile_mask, hub_owner, hub_rows)

    def per_sample(sample_pair):
        return one_sample(sample_pair[0], sample_pair[1], conv_weight, mix_weight, graph)
    outs, grads, conv_parts, mix_parts = lax.map(per_sample, (jnp.moveaxis(signal, 1, 0), jnp.moveaxis(cotangent, 1, 0)))
    factor = 1.0 / math.sqrt(NODES * BATCH * T1)
    return (jnp.moveaxis(outs, 0, 1), jnp.moveaxis(grads, 0, 1), lax.optimization_barrier(jnp.sum(conv_parts, 0)) * factor, lax.optimization_barrier(jnp.sum(mix_parts, 0)) * factor)
```

```python
import functools
import math

import jax
import jax.numpy as jnp
from jax import lax
from jax.experimental import pallas as pl
from jax.experimental.pallas import tpu as pltpu
from jax.sharding import PartitionSpec as P

VMEM = pl.BlockSpec(memory_space=pltpu.VMEM)
SMEM = pl.BlockSpec(memory_space=pltpu.SMEM)
F32 = jnp.float32
BF16 = jnp.bfloat16


def nn(left, right):
    return lax.dot_general(left, right, (((1,), (0,)), ((), ())), preferred_element_type=F32)


def nt(left, right):
    return lax.dot_general(left, right, (((1,), (1,)), ((), ())), preferred_element_type=F32)


def tn(left, right):
    return lax.dot_general(left, right, (((0,), (0,)), ((), ())), preferred_element_type=F32)


def fill_taps(conv_ref, taps_ref):
    chans = conv_ref.shape[2]
    for kind in range(2):
        for tap in range(2):
            taps_ref[tap * chans : (tap + 1) * chans, kind * chans : (kind + 1) * chans] = conv_ref[
                kind, tap
            ]


def pre_kernel(
    row_ref,
    col_ref,
    keep_ref,
    sig_ref,
    cot_ref,
    conv_ref,
    mix_ref,
    tile_ref,
    pick_ref,
    place_ref,
    own_ref,
    far_ref,
    send_ref,
    hidden_ref,
    tanh_ref,
    gate_ref,
    back_ref,
    out_ref,
    dense_ref,
    taps_ref,
):
    nodes = own_ref.shape[0]
    tiles, block, _ = tile_ref.shape
    chans = conv_ref.shape[2]
    features = hidden_ref.shape[1]
    own_tiles = nodes // block
    all_tiles = dense_ref.shape[0]

    dense_ref[...] = jnp.zeros_like(dense_ref)
    for t in range(tiles):

        @pl.when(keep_ref[t] == 1)
        def _():
            rows = pl.ds(pl.multiple_of(row_ref[t] * block, block), block)
            dense_ref[col_ref[t], rows, :] += tile_ref[t].astype(F32)

    for c in range(own_tiles):
        own_ref[:, c * block : (c + 1) * block] = dense_ref[c].astype(BF16)
    slots = send_ref.shape[0]
    place = (
        place_ref[...] == lax.broadcasted_iota(jnp.int32, (place_ref.shape[0], slots), 1)
    ).astype(BF16)
    far = nn(dense_ref[own_tiles].astype(BF16), place[:block])
    for c in range(own_tiles + 1, all_tiles):
        at = (c - own_tiles) * block
        far += nn(dense_ref[c].astype(BF16), place[at : at + block])
    far_ref[...] = far.astype(BF16)
    send_ref[...] = (
        pick_ref[...] == lax.broadcasted_iota(jnp.int32, (slots, nodes), 1)
    ).astype(BF16)

    fill_taps(conv_ref, taps_ref)
    for t in range(features // chans):
        at = slice(t * chans, (t + 1) * chans)
        both = nn(sig_ref[:, t * chans : (t + 2) * chans], taps_ref[...])
        tanh_filt = jnp.tanh(both[:, :chans])
        sig_gate = jax.nn.sigmoid(both[:, chans:])
        tanh_ref[:, at] = tanh_filt
        gate_ref[:, at] = sig_gate
        hidden_ref[:, at] = (tanh_filt * sig_gate).astype(BF16)
        back_ref[:, at] = nt(cot_ref[:, at], mix_ref[2]).astype(BF16)
    out_ref[:, :features] = nn(send_ref[...], hidden_ref[...]).astype(BF16)
    out_ref[:, features:] = tn(far_ref[...], back_ref[...]).astype(BF16)


def mid_kernel(
    own_ref,
    far_ref,
    send_ref,
    hidden_ref,
    back_ref,
    cot_ref,
    mix_ref,
    in_ref,
    hop_ref,
    next_ref,
    out_ref,
):
    features = hidden_ref.shape[1]
    chans = mix_ref.shape[1]
    for t in range(features // chans):
        at = slice(t * chans, (t + 1) * chans)
        late = slice(features + t * chans, features + (t + 1) * chans)
        hop_ref[:, at] = (
            nn(own_ref[...], hidden_ref[:, at]) + nn(far_ref[...], in_ref[:, at])
        ).astype(BF16)
        next_ref[:, at] = (
            nt(cot_ref[:, at], mix_ref[1])
            + tn(own_ref[...], back_ref[:, at])
            + tn(send_ref[...], in_ref[:, late])
        ).astype(BF16)
    out_ref[:, :features] = nn(send_ref[...], hop_ref[...]).astype(BF16)
    out_ref[:, features:] = tn(far_ref[...], next_ref[...]).astype(BF16)


def post_kernel(
    own_ref,
    far_ref,
    send_ref,
    hidden_ref,
    hop_ref,
    back_ref,
    in_ref,
    sig_ref,
    cot_ref,
    tanh_ref,
    gate_ref,
    conv_ref,
    mix_ref,
    layer_ref,
    grad_ref,
    weight_ref,
    taps_ref,
    last_ref,
    held_ref,
):
    features = hidden_ref.shape[1]
    chans = mix_ref.shape[1]
    steps = features // chans
    fill_taps(conv_ref, taps_ref)
    for t in range(steps):
        at = slice(t * chans, (t + 1) * chans)
        after = slice((t + 1) * chans, (t + 2) * chans)
        late = slice(features + t * chans, features + (t + 1) * chans)
        cot = cot_ref[:, at]
        last_ref[...] = (
            nn(own_ref[...], hop_ref[:, at]) + nn(far_ref[...], in_ref[:, at])
        ).astype(BF16)
        layer_ref[:, at] = (
            sig_ref[:, after].astype(F32)
            + nn(hidden_ref[:, at], mix_ref[0])
            + nn(hop_ref[:, at], mix_ref[1])
            + nn(last_ref[...], mix_ref[2])
        ).astype(BF16)
        for k, source in enumerate((hidden_ref[:, at], hop_ref[:, at], last_ref[...])):
            part = tn(source, cot)
            place = slice((4 + k) * chans, (5 + k) * chans)
            weight_ref[place, :] = part if t == 0 else weight_ref[place, :] + part
        grad_hidden = (
            nt(cot, mix_ref[0])
            + tn(own_ref[...], back_ref[:, at])
            + tn(send_ref[...], in_ref[:, late])
        )
        tanh_filt = tanh_ref[:, at]
        sig_gate = gate_ref[:, at]
        held_ref[:, :chans] = (
            grad_hidden * sig_gate * (1.0 - tanh_filt * tanh_filt)
        ).astype(BF16)
        held_ref[:, chans:] = (grad_hidden * tanh_filt * sig_gate * (1.0 - sig_gate)).astype(BF16)
        outer = tn(sig_ref[:, t * chans : (t + 2) * chans], held_ref[...])
        for kind in range(2):
            for tap in range(2):
                part = outer[tap * chans : (tap + 1) * chans, kind * chans : (kind + 1) * chans]
                spot = (kind * 2 + tap) * chans
                place = slice(spot, spot + chans)
                weight_ref[place, :] = part if t == 0 else weight_ref[place, :] + part
        into = nt(held_ref[...], taps_ref[...])
        early = into[:, :chans]
        if t > 0:
            early = early + carried
        grad_ref[:, at] = early.astype(BF16)
        carried = into[:, chans:] + cot.astype(F32)
    grad_ref[:, features:] = carried.astype(BF16)


def stages_of(axis_sizes):
    bits = {}
    for axis, size in axis_sizes:
        bit = 1
        while bit < size:
            bits.setdefault(axis, []).append((axis, bit))
            bit *= 2
    return bits


def colours_of(bits, rows, chans):
    dom, batch = bits["dom"], bits["batch"]
    first, far = batch[:1], batch[1:]
    near, high = dom[:1], dom[1:]
    orders = (
        first + far + near + high,
        first + near + high + far,
        first + high + far + near,
    )
    units = rows // chans
    shares = [units - 2 * (units // 3), units // 3, units // 3]
    colours, base = [], 0
    for order, share in zip(orders, shares):
        plan, count = [], share * chans
        for axis, bit in order:
            halve = (count // 2) % 8 == 0
            plan.append((axis, bit, halve, count // 2 if halve else count))
            if halve:
                count //= 2
        colours.append((base, share * chans, plan))
        base += share * chans
    return colours


def partner_of(axis, bit):
    index = lax.axis_index(axis)
    mine = (index // bit) % 2
    return mine, index + bit - 2 * bit * mine


def reduce_kernel(
    colours, factor, grads_ref, out_ref, total, landing, send_sem, recv_sem, back_send, back_recv
):
    barrier = pltpu.get_barrier_semaphore()
    peers = sorted({(axis, bit) for axis, bit, _, _ in colours[0][2]})
    for axis, bit in peers:
        _, other = partner_of(axis, bit)
        pl.semaphore_signal(
            barrier, inc=1, device_id={axis: other}, device_id_type=pl.DeviceIdType.MESH
        )
    pl.semaphore_wait(barrier, len(peers))

    starts = [base for base, _, _ in colours]
    trail = [[] for _ in colours]
    landed = 0
    for s in range(len(colours[0][2])):
        moves = []
        for c, (_, _, plan) in enumerate(colours):
            axis, bit, halve, count = plan[s]
            mine, other = partner_of(axis, bit)
            source = grads_ref if s == 0 else total
            keep = starts[c] + mine * count if halve else starts[c]
            give = starts[c] + (1 - mine) * count if halve else starts[c]
            give_rows = pl.ds(pl.multiple_of(give, 8), count)
            keep_rows = pl.ds(pl.multiple_of(keep, 8), count)
            copy = pltpu.make_async_remote_copy(
                src_ref=source.at[give_rows],
                dst_ref=landing.at[pl.ds(landed, count)],
                send_sem=send_sem.at[c, s],
                recv_sem=recv_sem.at[c, s],
                device_id={axis: other},
                device_id_type=pl.DeviceIdType.MESH,
            )
            copy.start()
            moves.append((copy, source, keep_rows, landed, count))
            landed += count
            trail[c].append(keep)
            starts[c] = keep
        for copy, source, keep_rows, at, count in moves:
            copy.wait()
            total[keep_rows, :] = source[keep_rows, :] + landing[at : at + count, :]

    counts = []
    for c, (_, _, plan) in enumerate(colours):
        count = plan[-1][3]
        rows = pl.ds(pl.multiple_of(starts[c], 8), count)
        out_ref[rows, :] = total[rows, :] * factor
        counts.append(count)
    depth = len(colours[0][2])
    for s in range(depth - 1, -1, -1):
        moves = []
        for c, (_, _, plan) in enumerate(colours):
            axis, bit, halve, count = plan[s]
            if not halve:
                continue
            _, other = partner_of(axis, bit)
            rows = pl.ds(pl.multiple_of(trail[c][s], 8), count)
            copy = pltpu.make_async_remote_copy(
                src_ref=out_ref.at[rows],
                dst_ref=out_ref.at[rows],
                send_sem=back_send.at[c, s],
                recv_sem=back_recv.at[c, s],
                device_id={axis: other},
                device_id_type=pl.DeviceIdType.MESH,
            )
            copy.start()
            moves.append(copy)
        for copy in moves:
            copy.wait()


def reduce_weights(grads, axis_sizes, factor, chans):
    rows, lanes = grads.shape
    colours = colours_of(stages_of(axis_sizes), rows, chans)
    depth = len(colours[0][2])
    landing = sum(count for _, _, plan in colours for _, _, _, count in plan)
    sems = pltpu.SemaphoreType.DMA((len(colours), depth))
    return pl.pallas_call(
        functools.partial(reduce_kernel, colours, factor),
        out_shape=jax.ShapeDtypeStruct((rows, lanes), F32),
        in_specs=[VMEM],
        out_specs=VMEM,
        scratch_shapes=[
            pltpu.VMEM((rows, lanes), F32),
            pltpu.VMEM((landing, lanes), F32),
            sems,
            sems,
            sems,
            sems,
        ],
        compiler_params=pltpu.CompilerParams(collective_id=0, has_side_effects=True),
        name="reduce_weights",
    )(grads)


def shape_of(*dims, dtype=BF16):
    return jax.ShapeDtypeStruct(dims, dtype)


def body(
    axis_sizes,
    signal,
    cotangent,
    conv_weight,
    mix_weight,
    send_rows,
    send_mask,
    tile_vals,
    tile_row,
    tile_col,
    tile_mask,
    hub_owner,
    hub_rows,
):
    nodes, b_dev, steps, chans = signal.shape
    out_steps = steps - 1
    features = out_steps * chans
    n_dom, cap = send_rows.shape
    hub_per = hub_rows.shape[1]
    width = cap + hub_per
    slots = n_dom * width
    block = tile_vals.shape[1]
    all_tiles = (nodes + n_dom * cap + hub_rows.size) // block
    me = lax.axis_index("dom")

    sig = signal.reshape(nodes, steps * chans)
    cot = cotangent.reshape(nodes, features)

    mine = hub_owner == me
    own_hub = jnp.sum(jnp.where(mine[:, None], hub_rows + 1, 0), axis=0) - 1
    pick = jnp.concatenate(
        [
            jnp.where(send_mask == 1, send_rows, -1),
            jnp.broadcast_to(own_hub[None, :], (n_dom, hub_per)),
        ],
        axis=1,
    ).reshape(slots, 1)
    place = jnp.concatenate(
        [
            (
                jnp.arange(n_dom, dtype=jnp.int32)[:, None] * width
                + jnp.arange(cap, dtype=jnp.int32)[None, :]
            ).reshape(-1, 1),
            (
                hub_owner[:, None] * width + cap + jnp.arange(hub_per, dtype=jnp.int32)[None, :]
            ).reshape(-1, 1),
        ],
        axis=0,
    )

    own, far, send, hidden, tanh_filt, sig_gate, back_two, out_one = pl.pallas_call(
        pre_kernel,
        out_shape=(
            shape_of(nodes, nodes),
            shape_of(nodes, slots),
            shape_of(slots, nodes),
            shape_of(nodes, features),
            shape_of(nodes, features, dtype=F32),
            shape_of(nodes, features, dtype=F32),
            shape_of(nodes, features),
            shape_of(slots, 2 * features),
        ),
        in_specs=[SMEM] * 3 + [VMEM] * 7,
        out_specs=(VMEM,) * 8,
        scratch_shapes=[
            pltpu.VMEM((all_tiles, nodes, block), F32),
            pltpu.VMEM((2 * chans, 2 * chans), BF16),
        ],
        name="pre",
    )(tile_row, tile_col, tile_mask, sig, cot, conv_weight, mix_weight, tile_vals, pick, place)

    in_one = lax.all_to_all(out_one, "dom", split_axis=0, concat_axis=0, tiled=True)
    hop_one, back_one, out_two = pl.pallas_call(
        mid_kernel,
        out_shape=(
            shape_of(nodes, features),
            shape_of(nodes, features),
            shape_of(slots, 2 * features),
        ),
        in_specs=[VMEM] * 8,
        out_specs=(VMEM,) * 3,
        name="mid",
    )(own, far, send, hidden, back_two, cot, mix_weight, in_one)
    in_two = lax.all_to_all(out_two, "dom", split_axis=0, concat_axis=0, tiled=True)
    layer_out, signal_grad, grads = pl.pallas_call(
        post_kernel,
        out_shape=(
            shape_of(nodes, features),
            shape_of(nodes, steps * chans),
            shape_of(7 * chans, chans, dtype=F32),
        ),
        in_specs=[VMEM] * 13,
        out_specs=(VMEM,) * 3,
        scratch_shapes=[
            pltpu.VMEM((2 * chans, 2 * chans), BF16),
            pltpu.VMEM((nodes, chans), BF16),
            pltpu.VMEM((nodes, 2 * chans), BF16),
        ],
        name="post",
    )(
        own,
        far,
        send,
        hidden,
        hop_one,
        back_one,
        in_two,
        sig,
        cot,
        tanh_filt,
        sig_gate,
        conv_weight,
        mix_weight,
    )
    total_count = nodes * out_steps * b_dev
    for _, size in axis_sizes:
        total_count *= size
    reduced = reduce_weights(grads, axis_sizes, 1.0 / math.sqrt(total_count), chans)
    return (
        layer_out.reshape(nodes, b_dev, out_steps, chans),
        signal_grad.reshape(signal.shape),
        reduced[: 4 * chans].reshape(conv_weight.shape),
        reduced[4 * chans :].reshape(mix_weight.shape),
    )


def solution(mesh):
    placed = (
        P("dom", "batch", None, None),
        P("dom", "batch", None, None),
        P(),
        P(),
        P("dom", None),
        P("dom", None),
        P("dom", None, None),
        P("dom"),
        P("dom"),
        P("dom"),
        P(),
        P(),
    )
    axis_sizes = tuple((axis, mesh.shape[axis]) for axis in ("dom", "batch"))
    return jax.shard_map(
        functools.partial(body, axis_sizes),
        mesh=mesh,
        in_specs=placed,
        out_specs=(P("dom", "batch", None, None), P("dom", "batch", None, None), P(), P()),
        check_vma=False,
    )
```

```python
import functools
import math

import jax
import jax.numpy as jnp
import numpy as np
from jax import lax
from jax.experimental import pallas as pl
from jax.experimental.pallas import tpu as pltpu
from jax.sharding import PartitionSpec as P

VMEM = pl.BlockSpec(memory_space=pltpu.VMEM)
SMEM = pl.BlockSpec(memory_space=pltpu.SMEM)
F32 = jnp.float32
BF16 = jnp.bfloat16


def nn(left, right):
    return lax.dot_general(left, right, (((1,), (0,)), ((), ())), preferred_element_type=F32)


def nt(left, right):
    return lax.dot_general(left, right, (((1,), (1,)), ((), ())), preferred_element_type=F32)


def tn(left, right):
    return lax.dot_general(left, right, (((0,), (0,)), ((), ())), preferred_element_type=F32)


def fill_taps(conv_ref, taps_ref):
    chans = conv_ref.shape[2]
    for kind in range(2):
        for tap in range(2):
            taps_ref[tap * chans : (tap + 1) * chans, kind * chans : (kind + 1) * chans] = conv_ref[
                kind, tap
            ]


def pre_kernel(
    row_ref,
    col_ref,
    keep_ref,
    sig_ref,
    cot_ref,
    conv_ref,
    mix_ref,
    tile_ref,
    owner_ref,
    rows_ref,
    flag_ref,
    hubs_ref,
    expand_ref,
    lane_ref,
    halo_ref,
    own_ref,
    far_ref,
    send_ref,
    hidden_ref,
    tanh_ref,
    gate_ref,
    back_ref,
    out_ref,
    dense_ref,
    place_ref,
    taps_ref,
):
    nodes = own_ref.shape[0]
    tiles, block, _ = tile_ref.shape
    chans = conv_ref.shape[2]
    features = hidden_ref.shape[1]
    own_tiles = nodes // block
    all_tiles = dense_ref.shape[0]

    dense_ref[...] = jnp.zeros_like(dense_ref)
    for t in range(tiles):

        @pl.when(keep_ref[t] == 1)
        def _():
            rows = pl.ds(pl.multiple_of(row_ref[t] * block, block), block)
            dense_ref[col_ref[t], rows, :] += tile_ref[t].astype(F32)

    for c in range(own_tiles):
        own_ref[:, c * block : (c + 1) * block] = dense_ref[c].astype(BF16)
    slots = send_ref.shape[0]
    cap = rows_ref.shape[1]
    groups, hub_per = hubs_ref.shape
    width = cap + hub_per
    halo = halo_ref.shape[0]
    place_ref[:halo, :] = halo_ref[...]
    slot = lax.broadcasted_iota(jnp.int32, (hub_per, slots), 1)
    entry = lax.broadcasted_iota(jnp.int32, (hub_per, slots), 0) + cap
    me = lax.axis_index("dom")
    hub = jnp.zeros((1, hub_per), F32)
    for o in range(groups):
        at = halo + o * hub_per
        owner = owner_ref[o]
        place_ref[at : at + hub_per, :] = jnp.where(slot == entry + owner * width, 1.0, 0.0).astype(
            BF16
        )
        owned = (owner == me).astype(F32)
        hub += owned * (hubs_ref[o : o + 1, :].astype(F32) + 1.0)
    far = nn(dense_ref[own_tiles].astype(BF16), place_ref[:block, :])
    for c in range(own_tiles + 1, all_tiles):
        at = (c - own_tiles) * block
        far += nn(dense_ref[c].astype(BF16), place_ref[at : at + block, :])
    far_ref[...] = far.astype(BF16)
    chosen = jnp.where(flag_ref[...] == 1, rows_ref[...].astype(F32) + 1.0, 0.0)
    spread = jnp.dot(
        expand_ref[...], chosen, precision=lax.Precision.HIGHEST, preferred_element_type=F32
    )
    lane = lane_ref[...]
    from_halo = jnp.where(
        lax.broadcasted_iota(jnp.int32, (slots, cap), 1) == lane, spread, 0.0
    )
    from_hub = jnp.where(
        lax.broadcasted_iota(jnp.int32, (slots, hub_per), 1) + cap == lane,
        jnp.broadcast_to(hub, (slots, hub_per)),
        0.0,
    )
    pick = jnp.sum(from_halo, axis=1, keepdims=True) + jnp.sum(from_hub, axis=1, keepdims=True)
    pick = (pick + 0.5).astype(jnp.int32) - 1
    send_ref[...] = jnp.where(
        pick == lax.broadcasted_iota(jnp.int32, (slots, nodes), 1), 1.0, 0.0
    ).astype(BF16)

    fill_taps(conv_ref, taps_ref)
    for t in range(features // chans):
        at = slice(t * chans, (t + 1) * chans)
        both = nn(sig_ref[:, t * chans : (t + 2) * chans], taps_ref[...])
        tanh_filt = jnp.tanh(both[:, :chans])
        sig_gate = jax.nn.sigmoid(both[:, chans:])
        tanh_ref[:, at] = tanh_filt
        gate_ref[:, at] = sig_gate
        hidden_ref[:, at] = (tanh_filt * sig_gate).astype(BF16)
        back_ref[:, at] = nt(cot_ref[t], mix_ref[2]).astype(BF16)
    out_ref[:, :features] = nn(send_ref[...], hidden_ref[...]).astype(BF16)
    out_ref[:, features:] = tn(far_ref[...], back_ref[...]).astype(BF16)


def mid_kernel(
    own_ref,
    far_ref,
    send_ref,
    hidden_ref,
    back_ref,
    cot_ref,
    mix_ref,
    in_ref,
    hop_ref,
    next_ref,
    out_ref,
):
    features = hidden_ref.shape[1]
    chans = mix_ref.shape[1]
    for t in range(features // chans):
        at = slice(t * chans, (t + 1) * chans)
        late = slice(features + t * chans, features + (t + 1) * chans)
        hop_ref[:, at] = (
            nn(own_ref[...], hidden_ref[:, at]) + nn(far_ref[...], in_ref[:, at])
        ).astype(BF16)
        next_ref[:, at] = (
            nt(cot_ref[t], mix_ref[1])
            + tn(own_ref[...], back_ref[:, at])
            + tn(send_ref[...], in_ref[:, late])
        ).astype(BF16)
    out_ref[:, :features] = nn(send_ref[...], hop_ref[...]).astype(BF16)
    out_ref[:, features:] = tn(far_ref[...], next_ref[...]).astype(BF16)


def post_kernel(
    own_ref,
    far_ref,
    send_ref,
    hidden_ref,
    hop_ref,
    back_ref,
    in_ref,
    sig_ref,
    cot_ref,
    tanh_ref,
    gate_ref,
    conv_ref,
    mix_ref,
    layer_ref,
    grad_ref,
    weight_ref,
    taps_ref,
    last_ref,
    held_ref,
):
    features = hidden_ref.shape[1]
    chans = mix_ref.shape[1]
    steps = features // chans
    fill_taps(conv_ref, taps_ref)
    for t in range(steps):
        at = slice(t * chans, (t + 1) * chans)
        after = slice((t + 1) * chans, (t + 2) * chans)
        late = slice(features + t * chans, features + (t + 1) * chans)
        cot = cot_ref[t]
        last_ref[...] = (
            nn(own_ref[...], hop_ref[:, at]) + nn(far_ref[...], in_ref[:, at])
        ).astype(BF16)
        layer_ref[t] = (
            sig_ref[:, after].astype(F32)
            + nn(hidden_ref[:, at], mix_ref[0])
            + nn(hop_ref[:, at], mix_ref[1])
            + nn(last_ref[...], mix_ref[2])
        ).astype(BF16)
        for k, source in enumerate((hidden_ref[:, at], hop_ref[:, at], last_ref[...])):
            part = tn(source, cot)
            place = slice((4 + k) * chans, (5 + k) * chans)
            weight_ref[place, :] = part if t == 0 else weight_ref[place, :] + part
        grad_hidden = (
            nt(cot, mix_ref[0])
            + tn(own_ref[...], back_ref[:, at])
            + tn(send_ref[...], in_ref[:, late])
        )
        tanh_filt = tanh_ref[:, at]
        sig_gate = gate_ref[:, at]
        held_ref[:, :chans] = (
            grad_hidden * sig_gate * (1.0 - tanh_filt * tanh_filt)
        ).astype(BF16)
        held_ref[:, chans:] = (grad_hidden * tanh_filt * sig_gate * (1.0 - sig_gate)).astype(BF16)
        outer = tn(sig_ref[:, t * chans : (t + 2) * chans], held_ref[...])
        for kind in range(2):
            for tap in range(2):
                part = outer[tap * chans : (tap + 1) * chans, kind * chans : (kind + 1) * chans]
                spot = (kind * 2 + tap) * chans
                place = slice(spot, spot + chans)
                weight_ref[place, :] = part if t == 0 else weight_ref[place, :] + part
        into = nt(held_ref[...], taps_ref[...])
        early = into[:, :chans]
        if t > 0:
            early = early + carried
        grad_ref[:, at] = early.astype(BF16)
        carried = into[:, chans:] + cot.astype(F32)
    grad_ref[:, features:] = carried.astype(BF16)


def stages_of(axis_sizes):
    bits = {}
    for axis, size in axis_sizes:
        bit = 1
        while bit < size:
            bits.setdefault(axis, []).append((axis, bit))
            bit *= 2
    return bits


def colours_of(bits, rows, chans):
    dom, batch = bits["dom"], bits["batch"]
    first, far = batch[:1], batch[1:]
    near, high = dom[:1], dom[1:]
    orders = (
        first + far + near + high,
        first + near + high + far,
        first + high + far + near,
    )
    units = rows // chans
    shares = [units - 2 * (units // 3), units // 3, units // 3]
    colours, base = [], 0
    for order, share in zip(orders, shares):
        plan, count = [], share * chans
        for axis, bit in order:
            halve = (count // 2) % 16 == 0
            plan.append((axis, bit, halve, count // 2 if halve else count))
            if halve:
                count //= 2
        colours.append((base, share * chans, plan))
        base += share * chans
    return colours


def partner_of(axis, bit):
    index = lax.axis_index(axis)
    mine = (index // bit) % 2
    return mine, index + bit - 2 * bit * mine


def narrow(stage):
    return stage in (1, 2)


def landing_rows(colours, wanted):
    return sum(
        count
        for _, _, plan in colours
        for stage, (_, _, _, count) in enumerate(plan)
        if narrow(stage) == wanted
    )


def reduce_kernel(
    colours,
    factor,
    grads_ref,
    out_ref,
    total,
    wide,
    landed,
    leaving,
    send_sem,
    recv_sem,
    back_send,
    back_recv,
):
    barrier = pltpu.get_barrier_semaphore()
    peers = sorted({(axis, bit) for axis, bit, _, _ in colours[0][2]})
    for axis, bit in peers:
        _, other = partner_of(axis, bit)
        pl.semaphore_signal(
            barrier, inc=1, device_id={axis: other}, device_id_type=pl.DeviceIdType.MESH
        )
    pl.semaphore_wait(barrier, len(peers))

    starts = [base for base, _, _ in colours]
    trail = [[] for _ in colours]
    used = {True: 0, False: 0}
    depth = len(colours[0][2])
    for s in range(depth):
        moves = []
        small = narrow(s)
        landing = landed if small else wide
        for c, (_, _, plan) in enumerate(colours):
            axis, bit, halve, count = plan[s]
            mine, other = partner_of(axis, bit)
            source = grads_ref if s == 0 else total
            keep = starts[c] + mine * count if halve else starts[c]
            give = starts[c] + (1 - mine) * count if halve else starts[c]
            give_rows = pl.ds(pl.multiple_of(give, 16), count)
            keep_rows = pl.ds(pl.multiple_of(keep, 16), count)
            spot = pl.ds(used[small], count)
            if small:
                leaving[spot, :] = source[give_rows, :].astype(BF16)
            copy = pltpu.make_async_remote_copy(
                src_ref=leaving.at[spot] if small else source.at[give_rows],
                dst_ref=landing.at[spot],
                send_sem=send_sem.at[c, s],
                recv_sem=recv_sem.at[c, s],
                device_id={axis: other},
                device_id_type=pl.DeviceIdType.MESH,
            )
            copy.start()
            moves.append((copy, source, keep_rows, spot))
            used[small] += count
            trail[c].append(keep)
            starts[c] = keep
        for copy, source, keep_rows, spot in moves:
            copy.wait()
            total[keep_rows, :] = source[keep_rows, :] + landing[spot, :].astype(F32)

    for c, (_, _, plan) in enumerate(colours):
        rows = pl.ds(pl.multiple_of(starts[c], 16), plan[-1][3])
        out_ref[rows, :] = (total[rows, :] * factor).astype(BF16)
    for s in range(depth - 1, -1, -1):
        moves = []
        for c, (_, _, plan) in enumerate(colours):
            axis, bit, halve, count = plan[s]
            if not halve:
                continue
            _, other = partner_of(axis, bit)
            rows = pl.ds(pl.multiple_of(trail[c][s], 16), count)
            copy = pltpu.make_async_remote_copy(
                src_ref=out_ref.at[rows],
                dst_ref=out_ref.at[rows],
                send_sem=back_send.at[c, s],
                recv_sem=back_recv.at[c, s],
                device_id={axis: other},
                device_id_type=pl.DeviceIdType.MESH,
            )
            copy.start()
            moves.append(copy)
        for copy in moves:
            copy.wait()


def reduce_weights(grads, axis_sizes, factor, chans):
    rows, lanes = grads.shape
    colours = colours_of(stages_of(axis_sizes), rows, chans)
    sems = pltpu.SemaphoreType.DMA((len(colours), len(colours[0][2])))
    slim = landing_rows(colours, True)
    return pl.pallas_call(
        functools.partial(reduce_kernel, colours, factor),
        out_shape=jax.ShapeDtypeStruct((rows, lanes), BF16),
        in_specs=[VMEM],
        out_specs=VMEM,
        scratch_shapes=[
            pltpu.VMEM((rows, lanes), F32),
            pltpu.VMEM((landing_rows(colours, False), lanes), F32),
            pltpu.VMEM((slim, lanes), BF16),
            pltpu.VMEM((slim, lanes), BF16),
            sems,
            sems,
            sems,
            sems,
        ],
        compiler_params=pltpu.CompilerParams(collective_id=0, has_side_effects=True),
        name="reduce_weights",
    )(grads)


def shape_of(*dims, dtype=BF16):
    return jax.ShapeDtypeStruct(dims, dtype)


def body(
    axis_sizes,
    signal,
    cotangent,
    conv_weight,
    mix_weight,
    send_rows,
    send_mask,
    tile_vals,
    tile_row,
    tile_col,
    tile_mask,
    hub_owner,
    hub_rows,
):
    nodes, b_dev, steps, chans = signal.shape
    out_steps = steps - 1
    features = out_steps * chans
    n_dom, cap = send_rows.shape
    hub_per = hub_rows.shape[1]
    width = cap + hub_per
    slots = n_dom * width
    block = tile_vals.shape[1]
    all_tiles = (nodes + n_dom * cap + hub_rows.size) // block

    sig = signal.reshape(nodes, steps * chans)
    cot = jnp.transpose(cotangent.reshape(nodes, out_steps, chans), (1, 0, 2))

    slot = np.arange(slots)
    expand = (slot[:, None] // width == np.arange(n_dom)[None, :]).astype(np.float32)
    lane = (slot % width).astype(np.int32)[:, None]
    entry = np.arange(n_dom * cap)
    halo = jnp.asarray(
        (entry // cap * width + entry % cap)[:, None] == slot[None, :], dtype=BF16
    )

    own, far, send, hidden, tanh_filt, sig_gate, back_two, out_one = pl.pallas_call(
        pre_kernel,
        out_shape=(
            shape_of(nodes, nodes),
            shape_of(nodes, slots),
            shape_of(slots, nodes),
            shape_of(nodes, features),
            shape_of(nodes, features, dtype=F32),
            shape_of(nodes, features, dtype=F32),
            shape_of(nodes, features),
            shape_of(slots, 2 * features),
        ),
        in_specs=[SMEM] * 3 + [VMEM] * 5 + [SMEM] + [VMEM] * 6,
        out_specs=(VMEM,) * 8,
        scratch_shapes=[
            pltpu.VMEM((all_tiles, nodes, block), F32),
            pltpu.VMEM((n_dom * cap + hub_rows.size, slots), BF16),
            pltpu.VMEM((2 * chans, 2 * chans), BF16),
        ],
        name="pre",
    )(
        tile_row,
        tile_col,
        tile_mask,
        sig,
        cot,
        conv_weight,
        mix_weight,
        tile_vals,
        hub_owner,
        send_rows,
        send_mask,
        hub_rows,
        expand,
        lane,
        halo,
    )

    in_one = lax.all_to_all(out_one, "dom", split_axis=0, concat_axis=0, tiled=True)
    hop_one, back_one, out_two = pl.pallas_call(
        mid_kernel,
        out_shape=(
            shape_of(nodes, features),
            shape_of(nodes, features),
            shape_of(slots, 2 * features),
        ),
        in_specs=[VMEM] * 8,
        out_specs=(VMEM,) * 3,
        name="mid",
    )(own, far, send, hidden, back_two, cot, mix_weight, in_one)
    in_two = lax.all_to_all(out_two, "dom", split_axis=0, concat_axis=0, tiled=True)
    layer_out, signal_grad, grads = pl.pallas_call(
        post_kernel,
        out_shape=(
            shape_of(out_steps, nodes, chans),
            shape_of(nodes, steps * chans),
            shape_of(7 * chans, chans, dtype=F32),
        ),
        in_specs=[VMEM] * 13,
        out_specs=(VMEM,) * 3,
        scratch_shapes=[
            pltpu.VMEM((2 * chans, 2 * chans), BF16),
            pltpu.VMEM((nodes, chans), BF16),
            pltpu.VMEM((nodes, 2 * chans), BF16),
        ],
        name="post",
    )(
        own,
        far,
        send,
        hidden,
        hop_one,
        back_one,
        in_two,
        sig,
        cot,
        tanh_filt,
        sig_gate,
        conv_weight,
        mix_weight,
    )
    total_count = nodes * out_steps * b_dev
    for _, size in axis_sizes:
        total_count *= size
    reduced = reduce_weights(grads, axis_sizes, 1.0 / math.sqrt(total_count), chans)
    return (
        jnp.transpose(layer_out, (1, 0, 2)).reshape(nodes, b_dev, out_steps, chans),
        signal_grad.reshape(signal.shape),
        reduced[: 4 * chans].astype(F32).reshape(conv_weight.shape),
        reduced[4 * chans :].astype(F32).reshape(mix_weight.shape),
    )


def solution(mesh):
    placed = (
        P("dom", "batch", None, None),
        P("dom", "batch", None, None),
        P(),
        P(),
        P("dom", None),
        P("dom", None),
        P("dom", None, None),
        P("dom"),
        P("dom"),
        P("dom"),
        P(),
        P(),
    )
    axis_sizes = tuple((axis, mesh.shape[axis]) for axis in ("dom", "batch"))
    return jax.shard_map(
        functools.partial(body, axis_sizes),
        mesh=mesh,
        in_specs=placed,
        out_specs=(P("dom", "batch", None, None), P("dom", "batch", None, None), P(), P()),
        check_vma=False,
    )
```

```python
import functools
import math

import jax
import jax.numpy as jnp
import numpy as np
from jax import lax
from jax.experimental import pallas as pl
from jax.experimental.pallas import tpu as pltpu
from jax.sharding import PartitionSpec as P

VMEM = pl.BlockSpec(memory_space=pltpu.VMEM)
SMEM = pl.BlockSpec(memory_space=pltpu.SMEM)
F32 = jnp.float32
BF16 = jnp.bfloat16


def nn(left, right):
    return lax.dot_general(left, right, (((1,), (0,)), ((), ())), preferred_element_type=F32)


def nt(left, right):
    return lax.dot_general(left, right, (((1,), (1,)), ((), ())), preferred_element_type=F32)


def tn(left, right):
    return lax.dot_general(left, right, (((0,), (0,)), ((), ())), preferred_element_type=F32)


def fill_taps(conv_ref, taps_ref):
    chans = conv_ref.shape[2]
    for kind in range(2):
        for tap in range(2):
            taps_ref[tap * chans : (tap + 1) * chans, kind * chans : (kind + 1) * chans] = conv_ref[
                kind, tap
            ]


def pre_kernel(
    row_ref,
    col_ref,
    keep_ref,
    sig_ref,
    cot_ref,
    conv_ref,
    mix_ref,
    tile_ref,
    owner_ref,
    rows_ref,
    flag_ref,
    hubs_ref,
    expand_ref,
    lane_ref,
    halo_ref,
    own_ref,
    far_ref,
    send_ref,
    hidden_ref,
    tanh_ref,
    gate_ref,
    back_ref,
    out_ref,
    dense_ref,
    place_ref,
    taps_ref,
):
    nodes = own_ref.shape[0]
    tiles, block, _ = tile_ref.shape
    chans = conv_ref.shape[2]
    features = hidden_ref.shape[1]
    own_tiles = nodes // block
    all_tiles = dense_ref.shape[0]

    dense_ref[...] = jnp.zeros_like(dense_ref)
    for t in range(tiles):

        @pl.when(keep_ref[t] == 1)
        def _():
            rows = pl.ds(pl.multiple_of(row_ref[t] * block, block), block)
            dense_ref[col_ref[t], rows, :] += tile_ref[t].astype(F32)

    for c in range(own_tiles):
        own_ref[:, c * block : (c + 1) * block] = dense_ref[c].astype(BF16)
    slots = send_ref.shape[0]
    cap = rows_ref.shape[1]
    groups, hub_per = hubs_ref.shape
    width = slots // expand_ref.shape[1]
    halo = halo_ref.shape[0]
    place_ref[:halo, :] = halo_ref[...]
    slot = lax.broadcasted_iota(jnp.int32, (hub_per, slots), 1)
    entry = lax.broadcasted_iota(jnp.int32, (hub_per, slots), 0) + cap
    me = lax.axis_index("dom")
    hub = jnp.zeros((1, hub_per), F32)
    for o in range(groups):
        at = halo + o * hub_per
        owner = owner_ref[o]
        place_ref[at : at + hub_per, :] = jnp.where(slot == entry + owner * width, 1.0, 0.0).astype(
            BF16
        )
        owned = (owner == me).astype(F32)
        hub += owned * (hubs_ref[o : o + 1, :].astype(F32) + 1.0)
    far = nn(dense_ref[own_tiles].astype(BF16), place_ref[:block, :])
    for c in range(own_tiles + 1, all_tiles):
        at = (c - own_tiles) * block
        far += nn(dense_ref[c].astype(BF16), place_ref[at : at + block, :])
    far_ref[...] = far.astype(BF16)
    chosen = jnp.where(flag_ref[...] == 1, rows_ref[...].astype(F32) + 1.0, 0.0)
    spread = jnp.dot(
        expand_ref[...], chosen, precision=lax.Precision.HIGHEST, preferred_element_type=F32
    )
    lane = lane_ref[...]
    from_halo = jnp.where(
        lax.broadcasted_iota(jnp.int32, (slots, cap), 1) == lane, spread, 0.0
    )
    from_hub = jnp.where(
        lax.broadcasted_iota(jnp.int32, (slots, hub_per), 1) + cap == lane,
        jnp.broadcast_to(hub, (slots, hub_per)),
        0.0,
    )
    pick = jnp.sum(from_halo, axis=1, keepdims=True) + jnp.sum(from_hub, axis=1, keepdims=True)
    pick = (pick + 0.5).astype(jnp.int32) - 1
    send_ref[...] = jnp.where(
        pick == lax.broadcasted_iota(jnp.int32, (slots, nodes), 1), 1.0, 0.0
    ).astype(BF16)

    fill_taps(conv_ref, taps_ref)
    for t in range(features // chans):
        at = slice(t * chans, (t + 1) * chans)
        both = nn(sig_ref[:, t * chans : (t + 2) * chans], taps_ref[...])
        tanh_filt = jnp.tanh(both[:, :chans])
        sig_gate = jax.nn.sigmoid(both[:, chans:])
        tanh_ref[:, at] = tanh_filt
        gate_ref[:, at] = sig_gate
        hidden_ref[:, at] = (tanh_filt * sig_gate).astype(BF16)
        back_ref[:, at] = nt(cot_ref[t], mix_ref[2]).astype(BF16)
    out_ref[:, :features] = nn(send_ref[...], hidden_ref[...]).astype(BF16)
    out_ref[:, features:] = tn(far_ref[...], back_ref[...]).astype(BF16)


def rows_of(index, width):
    return pl.ds(pl.multiple_of(index * width, 16), width)


def exchange(devices, out_ref, in_ref, send_sem, recv_sem):
    slots, lanes = out_ref.shape
    width = slots // devices
    half = lanes // 2
    me = lax.axis_index("dom")
    barrier = pltpu.get_barrier_semaphore()
    for d in range(1, devices):
        pl.semaphore_signal(
            barrier,
            inc=1,
            device_id={"dom": lax.rem(me + d, devices)},
            device_id_type=pl.DeviceIdType.MESH,
        )
    pl.semaphore_wait(barrier, devices - 1)
    groups = []
    for k, span in enumerate((slice(half, lanes), slice(0, half))):
        copies = []
        for d in range(1, devices):
            other = lax.rem(me + d, devices)
            copy = pltpu.make_async_remote_copy(
                src_ref=out_ref.at[rows_of(other, width), span],
                dst_ref=in_ref.at[rows_of(me, width), span],
                send_sem=send_sem.at[k, d - 1],
                recv_sem=recv_sem.at[k, d - 1],
                device_id={"dom": other},
                device_id_type=pl.DeviceIdType.MESH,
            )
            copy.start()
            copies.append(copy)
        groups.append(copies)
    in_ref[rows_of(me, width), :] = out_ref[rows_of(me, width), :]
    return groups


def mid_kernel(
    devices,
    own_ref,
    far_ref,
    send_ref,
    hidden_ref,
    back_ref,
    cot_ref,
    mix_ref,
    leave_ref,
    hop_ref,
    next_ref,
    out_ref,
    in_ref,
    hop_sum,
    next_sum,
    send_sem,
    recv_sem,
):
    features = hidden_ref.shape[1]
    chans = mix_ref.shape[1]
    spans = [slice(t * chans, (t + 1) * chans) for t in range(features // chans)]
    late, early = exchange(devices, leave_ref, in_ref, send_sem, recv_sem)
    for t, at in enumerate(spans):
        next_sum[:, at] = nt(cot_ref[t], mix_ref[1]) + tn(own_ref[...], back_ref[:, at])
        hop_sum[:, at] = nn(own_ref[...], hidden_ref[:, at])
    for copy in late:
        copy.wait_recv()
    next_ref[...] = (next_sum[...] + tn(send_ref[...], in_ref[:, features:])).astype(BF16)
    out_ref[:, features:] = tn(far_ref[...], next_ref[...]).astype(BF16)
    for copy in early:
        copy.wait_recv()
    hop_ref[...] = (hop_sum[...] + nn(far_ref[...], in_ref[:, :features])).astype(BF16)
    out_ref[:, :features] = nn(send_ref[...], hop_ref[...]).astype(BF16)
    for copy in late + early:
        copy.wait_send()


def post_kernel(
    devices,
    own_ref,
    far_ref,
    send_ref,
    hidden_ref,
    hop_ref,
    back_ref,
    leave_ref,
    sig_ref,
    cot_ref,
    tanh_ref,
    gate_ref,
    conv_ref,
    mix_ref,
    layer_ref,
    grad_ref,
    weight_ref,
    in_ref,
    hop_sum,
    layer_sum,
    hidden_sum,
    taps_ref,
    last_ref,
    held_ref,
    send_sem,
    recv_sem,
):
    features = hidden_ref.shape[1]
    chans = mix_ref.shape[1]
    spans = [slice(t * chans, (t + 1) * chans) for t in range(features // chans)]
    late, early = exchange(devices, leave_ref, in_ref, send_sem, recv_sem)

    def add_weight(spot, part, first):
        place = slice(spot * chans, (spot + 1) * chans)
        weight_ref[place, :] = part if first else weight_ref[place, :] + part

    fill_taps(conv_ref, taps_ref)
    for t, at in enumerate(spans):
        hidden_sum[:, at] = nt(cot_ref[t], mix_ref[0]) + tn(own_ref[...], back_ref[:, at])
        hop_sum[:, at] = nn(own_ref[...], hop_ref[:, at])
        layer_sum[:, at] = (
            sig_ref[:, (t + 1) * chans : (t + 2) * chans].astype(F32)
            + nn(hidden_ref[:, at], mix_ref[0])
            + nn(hop_ref[:, at], mix_ref[1])
        )
        add_weight(4, tn(hidden_ref[:, at], cot_ref[t]), t == 0)
        add_weight(5, tn(hop_ref[:, at], cot_ref[t]), t == 0)

    for copy in late:
        copy.wait_recv()
    for t, at in enumerate(spans):
        cot = cot_ref[t]
        grad_hidden = hidden_sum[:, at] + tn(
            send_ref[...], in_ref[:, features + t * chans : features + (t + 1) * chans]
        )
        tanh_filt = tanh_ref[:, at]
        sig_gate = gate_ref[:, at]
        held_ref[:, :chans] = (
            grad_hidden * sig_gate * (1.0 - tanh_filt * tanh_filt)
        ).astype(BF16)
        held_ref[:, chans:] = (grad_hidden * tanh_filt * sig_gate * (1.0 - sig_gate)).astype(BF16)
        outer = tn(sig_ref[:, t * chans : (t + 2) * chans], held_ref[...])
        for kind in range(2):
            for tap in range(2):
                part = outer[tap * chans : (tap + 1) * chans, kind * chans : (kind + 1) * chans]
                add_weight(kind * 2 + tap, part, t == 0)
        into = nt(held_ref[...], taps_ref[...])
        before = into[:, :chans]
        if t > 0:
            before = before + carried
        grad_ref[:, at] = before.astype(BF16)
        carried = into[:, chans:] + cot.astype(F32)
    grad_ref[:, features:] = carried.astype(BF16)

    for copy in early:
        copy.wait_recv()
    for t, at in enumerate(spans):
        last_ref[...] = (hop_sum[:, at] + nn(far_ref[...], in_ref[:, at])).astype(BF16)
        layer_ref[t] = (layer_sum[:, at] + nn(last_ref[...], mix_ref[2])).astype(BF16)
        add_weight(6, tn(last_ref[...], cot_ref[t]), t == 0)
    for copy in late + early:
        copy.wait_send()


def stages_of(axis_sizes):
    bits = {}
    for axis, size in axis_sizes:
        bit = 1
        while bit < size:
            bits.setdefault(axis, []).append((axis, bit))
            bit *= 2
    return bits


def colours_of(bits, rows, chans):
    dom, batch = bits["dom"], bits["batch"]
    first, far = batch[:1], batch[1:]
    near, high = dom[:1], dom[1:]
    orders = (
        first + far + near + high,
        first + near + high + far,
        first + high + far + near,
    )
    units = rows // chans
    shares = [units - 2 * (units // 3), units // 3, units // 3]
    colours, base = [], 0
    for order, share in zip(orders, shares):
        plan, count = [], share * chans
        for axis, bit in order:
            halve = (count // 2) % 16 == 0
            plan.append((axis, bit, halve, count // 2 if halve else count))
            if halve:
                count //= 2
        colours.append((base, share * chans, plan))
        base += share * chans
    return colours


def partner_of(axis, bit):
    index = lax.axis_index(axis)
    mine = (index // bit) % 2
    return mine, index + bit - 2 * bit * mine


def narrow(stage):
    return stage in (1, 2)


def landing_rows(colours, wanted):
    return sum(
        count
        for _, _, plan in colours
        for stage, (_, _, _, count) in enumerate(plan)
        if narrow(stage) == wanted
    )


def reduce_kernel(
    colours,
    factor,
    grads_ref,
    out_ref,
    total,
    wide,
    landed,
    leaving,
    send_sem,
    recv_sem,
    back_send,
    back_recv,
):
    barrier = pltpu.get_barrier_semaphore()
    peers = sorted({(axis, bit) for axis, bit, _, _ in colours[0][2]})
    for axis, bit in peers:
        _, other = partner_of(axis, bit)
        pl.semaphore_signal(
            barrier, inc=1, device_id={axis: other}, device_id_type=pl.DeviceIdType.MESH
        )
    pl.semaphore_wait(barrier, len(peers))

    starts = [base for base, _, _ in colours]
    trail = [[] for _ in colours]
    used = {True: 0, False: 0}
    depth = len(colours[0][2])
    for s in range(depth):
        moves = []
        small = narrow(s)
        landing = landed if small else wide
        for c, (_, _, plan) in enumerate(colours):
            axis, bit, halve, count = plan[s]
            mine, other = partner_of(axis, bit)
            source = grads_ref if s == 0 else total
            keep = starts[c] + mine * count if halve else starts[c]
            give = starts[c] + (1 - mine) * count if halve else starts[c]
            give_rows = pl.ds(pl.multiple_of(give, 16), count)
            keep_rows = pl.ds(pl.multiple_of(keep, 16), count)
            spot = pl.ds(used[small], count)
            if small:
                leaving[spot, :] = source[give_rows, :].astype(BF16)
            copy = pltpu.make_async_remote_copy(
                src_ref=leaving.at[spot] if small else source.at[give_rows],
                dst_ref=landing.at[spot],
                send_sem=send_sem.at[c, s],
                recv_sem=recv_sem.at[c, s],
                device_id={axis: other},
                device_id_type=pl.DeviceIdType.MESH,
            )
            copy.start()
            moves.append((copy, source, keep_rows, spot))
            used[small] += count
            trail[c].append(keep)
            starts[c] = keep
        for copy, source, keep_rows, spot in moves:
            copy.wait()
            total[keep_rows, :] = source[keep_rows, :] + landing[spot, :].astype(F32)

    for c, (_, _, plan) in enumerate(colours):
        rows = pl.ds(pl.multiple_of(starts[c], 16), plan[-1][3])
        out_ref[rows, :] = (total[rows, :] * factor).astype(BF16)
    for s in range(depth - 1, -1, -1):
        moves = []
        for c, (_, _, plan) in enumerate(colours):
            axis, bit, halve, count = plan[s]
            if not halve:
                continue
            _, other = partner_of(axis, bit)
            rows = pl.ds(pl.multiple_of(trail[c][s], 16), count)
            copy = pltpu.make_async_remote_copy(
                src_ref=out_ref.at[rows],
                dst_ref=out_ref.at[rows],
                send_sem=back_send.at[c, s],
                recv_sem=back_recv.at[c, s],
                device_id={axis: other},
                device_id_type=pl.DeviceIdType.MESH,
            )
            copy.start()
            moves.append(copy)
        for copy in moves:
            copy.wait()


def reduce_weights(grads, axis_sizes, factor, chans):
    rows, lanes = grads.shape
    colours = colours_of(stages_of(axis_sizes), rows, chans)
    sems = pltpu.SemaphoreType.DMA((len(colours), len(colours[0][2])))
    slim = landing_rows(colours, True)
    return pl.pallas_call(
        functools.partial(reduce_kernel, colours, factor),
        out_shape=jax.ShapeDtypeStruct((rows, lanes), BF16),
        in_specs=[VMEM],
        out_specs=VMEM,
        scratch_shapes=[
            pltpu.VMEM((rows, lanes), F32),
            pltpu.VMEM((landing_rows(colours, False), lanes), F32),
            pltpu.VMEM((slim, lanes), BF16),
            pltpu.VMEM((slim, lanes), BF16),
            sems,
            sems,
            sems,
            sems,
        ],
        compiler_params=pltpu.CompilerParams(collective_id=0, has_side_effects=True),
        name="reduce_weights",
    )(grads)


def shape_of(*dims, dtype=BF16):
    return jax.ShapeDtypeStruct(dims, dtype)


def body(
    axis_sizes,
    signal,
    cotangent,
    conv_weight,
    mix_weight,
    send_rows,
    send_mask,
    tile_vals,
    tile_row,
    tile_col,
    tile_mask,
    hub_owner,
    hub_rows,
):
    nodes, b_dev, steps, chans = signal.shape
    out_steps = steps - 1
    features = out_steps * chans
    n_dom, cap = send_rows.shape
    hub_per = hub_rows.shape[1]
    width = -(-(cap + hub_per) // 16) * 16
    slots = n_dom * width
    block = tile_vals.shape[1]
    all_tiles = (nodes + n_dom * cap + hub_rows.size) // block

    sig = signal.reshape(nodes, steps * chans)
    cot = jnp.transpose(cotangent.reshape(nodes, out_steps, chans), (1, 0, 2))

    slot = np.arange(slots)
    expand = (slot[:, None] // width == np.arange(n_dom)[None, :]).astype(np.float32)
    lane = (slot % width).astype(np.int32)[:, None]
    entry = np.arange(n_dom * cap)
    halo = jnp.asarray(
        (entry // cap * width + entry % cap)[:, None] == slot[None, :], dtype=BF16
    )

    own, far, send, hidden, tanh_filt, sig_gate, back_two, out_one = pl.pallas_call(
        pre_kernel,
        out_shape=(
            shape_of(nodes, nodes),
            shape_of(nodes, slots),
            shape_of(slots, nodes),
            shape_of(nodes, features),
            shape_of(nodes, features, dtype=F32),
            shape_of(nodes, features, dtype=F32),
            shape_of(nodes, features),
            shape_of(slots, 2 * features),
        ),
        in_specs=[SMEM] * 3 + [VMEM] * 5 + [SMEM] + [VMEM] * 6,
        out_specs=(VMEM,) * 8,
        scratch_shapes=[
            pltpu.VMEM((all_tiles, nodes, block), F32),
            pltpu.VMEM((n_dom * cap + hub_rows.size, slots), BF16),
            pltpu.VMEM((2 * chans, 2 * chans), BF16),
        ],
        name="pre",
    )(
        tile_row,
        tile_col,
        tile_mask,
        sig,
        cot,
        conv_weight,
        mix_weight,
        tile_vals,
        hub_owner,
        send_rows,
        send_mask,
        hub_rows,
        expand,
        lane,
        halo,
    )

    sems = pltpu.SemaphoreType.DMA((2, n_dom - 1))
    landing = pltpu.VMEM((slots, 2 * features), BF16)
    partial = pltpu.VMEM((nodes, features), F32)
    hop_one, back_one, out_two = pl.pallas_call(
        functools.partial(mid_kernel, n_dom),
        out_shape=(
            shape_of(nodes, features),
            shape_of(nodes, features),
            shape_of(slots, 2 * features),
        ),
        in_specs=[VMEM] * 8,
        out_specs=(VMEM,) * 3,
        scratch_shapes=[landing, partial, partial, sems, sems],
        compiler_params=pltpu.CompilerParams(collective_id=1, has_side_effects=True),
        name="mid",
    )(own, far, send, hidden, back_two, cot, mix_weight, out_one)
    layer_out, signal_grad, grads = pl.pallas_call(
        functools.partial(post_kernel, n_dom),
        out_shape=(
            shape_of(out_steps, nodes, chans),
            shape_of(nodes, steps * chans),
            shape_of(7 * chans, chans, dtype=F32),
        ),
        in_specs=[VMEM] * 13,
        out_specs=(VMEM,) * 3,
        scratch_shapes=[
            landing,
            partial,
            partial,
            partial,
            pltpu.VMEM((2 * chans, 2 * chans), BF16),
            pltpu.VMEM((nodes, chans), BF16),
            pltpu.VMEM((nodes, 2 * chans), BF16),
            sems,
            sems,
        ],
        compiler_params=pltpu.CompilerParams(collective_id=2, has_side_effects=True),
        name="post",
    )(
        own,
        far,
        send,
        hidden,
        hop_one,
        back_one,
        out_two,
        sig,
        cot,
        tanh_filt,
        sig_gate,
        conv_weight,
        mix_weight,
    )
    total_count = nodes * out_steps * b_dev
    for _, size in axis_sizes:
        total_count *= size
    reduced = reduce_weights(grads, axis_sizes, 1.0 / math.sqrt(total_count), chans)
    return (
        jnp.transpose(layer_out, (1, 0, 2)).reshape(nodes, b_dev, out_steps, chans),
        signal_grad.reshape(signal.shape),
        reduced[: 4 * chans].astype(F32).reshape(conv_weight.shape),
        reduced[4 * chans :].astype(F32).reshape(mix_weight.shape),
    )


def solution(mesh):
    placed = (
        P("dom", "batch", None, None),
        P("dom", "batch", None, None),
        P(),
        P(),
        P("dom", None),
        P("dom", None),
        P("dom", None, None),
        P("dom"),
        P("dom"),
        P("dom"),
        P(),
        P(),
    )
    axis_sizes = tuple((axis, mesh.shape[axis]) for axis in ("dom", "batch"))
    return jax.shard_map(
        functools.partial(body, axis_sizes),
        mesh=mesh,
        in_specs=placed,
        out_specs=(P("dom", "batch", None, None), P("dom", "batch", None, None), P(), P()),
        check_vma=False,
    )
```

```python
import functools
import math

import jax
import jax.numpy as jnp
import numpy as np
from jax import lax
from jax.experimental import pallas as pl
from jax.experimental.pallas import tpu as pltpu
from jax.sharding import PartitionSpec as P

VMEM = pl.BlockSpec(memory_space=pltpu.VMEM)
SMEM = pl.BlockSpec(memory_space=pltpu.SMEM)
F32 = jnp.float32
BF16 = jnp.bfloat16


def nn(left, right):
    return lax.dot_general(left, right, (((1,), (0,)), ((), ())), preferred_element_type=F32)


def nt(left, right):
    return lax.dot_general(left, right, (((1,), (1,)), ((), ())), preferred_element_type=F32)


def tn(left, right):
    return lax.dot_general(left, right, (((0,), (0,)), ((), ())), preferred_element_type=F32)


def fill_taps(conv_ref, taps_ref):
    chans = conv_ref.shape[2]
    for kind in range(2):
        for tap in range(2):
            taps_ref[tap * chans : (tap + 1) * chans, kind * chans : (kind + 1) * chans] = conv_ref[
                kind, tap
            ]


def pre_kernel(
    row_ref,
    col_ref,
    keep_ref,
    sig_ref,
    cot_ref,
    conv_ref,
    mix_ref,
    tile_ref,
    owner_ref,
    rows_ref,
    flag_ref,
    hubs_ref,
    expand_ref,
    lane_ref,
    halo_ref,
    own_ref,
    far_ref,
    send_ref,
    hidden_ref,
    tanh_ref,
    gate_ref,
    back_ref,
    out_ref,
    dense_ref,
    place_ref,
    taps_ref,
):
    nodes = own_ref.shape[0]
    tiles, block, _ = tile_ref.shape
    chans = conv_ref.shape[2]
    features = hidden_ref.shape[1]
    own_tiles = nodes // block
    all_tiles = dense_ref.shape[0]

    dense_ref[...] = jnp.zeros_like(dense_ref)
    for t in range(tiles):

        @pl.when(keep_ref[t] == 1)
        def _():
            rows = pl.ds(pl.multiple_of(row_ref[t] * block, block), block)
            dense_ref[col_ref[t], rows, :] += tile_ref[t].astype(F32)

    for c in range(own_tiles):
        own_ref[:, c * block : (c + 1) * block] = dense_ref[c].astype(BF16)
    slots = send_ref.shape[0]
    cap = rows_ref.shape[1]
    groups, hub_per = hubs_ref.shape
    width = slots // expand_ref.shape[1]
    halo = halo_ref.shape[0]
    place_ref[:halo, :] = halo_ref[...]
    slot = lax.broadcasted_iota(jnp.int32, (hub_per, slots), 1)
    entry = lax.broadcasted_iota(jnp.int32, (hub_per, slots), 0) + cap
    me = lax.axis_index("dom")
    hub = jnp.zeros((1, hub_per), F32)
    for o in range(groups):
        at = halo + o * hub_per
        owner = owner_ref[o]
        place_ref[at : at + hub_per, :] = jnp.where(slot == entry + owner * width, 1.0, 0.0).astype(
            BF16
        )
        owned = (owner == me).astype(F32)
        hub += owned * (hubs_ref[o : o + 1, :].astype(F32) + 1.0)
    far = nn(dense_ref[own_tiles].astype(BF16), place_ref[:block, :])
    for c in range(own_tiles + 1, all_tiles):
        at = (c - own_tiles) * block
        far += nn(dense_ref[c].astype(BF16), place_ref[at : at + block, :])
    far_ref[...] = far.astype(BF16)
    chosen = jnp.where(flag_ref[...] == 1, rows_ref[...].astype(F32) + 1.0, 0.0)
    spread = jnp.dot(
        expand_ref[...], chosen, precision=lax.Precision.HIGHEST, preferred_element_type=F32
    )
    lane = lane_ref[...]
    from_halo = jnp.where(
        lax.broadcasted_iota(jnp.int32, (slots, cap), 1) == lane, spread, 0.0
    )
    from_hub = jnp.where(
        lax.broadcasted_iota(jnp.int32, (slots, hub_per), 1) + cap == lane,
        jnp.broadcast_to(hub, (slots, hub_per)),
        0.0,
    )
    pick = jnp.sum(from_halo, axis=1, keepdims=True) + jnp.sum(from_hub, axis=1, keepdims=True)
    pick = (pick + 0.5).astype(jnp.int32) - 1
    send_ref[...] = jnp.where(
        pick == lax.broadcasted_iota(jnp.int32, (slots, nodes), 1), 1.0, 0.0
    ).astype(BF16)

    fill_taps(conv_ref, taps_ref)
    for t in range(features // chans):
        at = slice(t * chans, (t + 1) * chans)
        both = nn(sig_ref[:, t * chans : (t + 2) * chans], taps_ref[...])
        tanh_filt = jnp.tanh(both[:, :chans])
        sig_gate = jax.nn.sigmoid(both[:, chans:])
        tanh_ref[:, at] = tanh_filt
        gate_ref[:, at] = sig_gate
        hidden_ref[:, at] = (tanh_filt * sig_gate).astype(BF16)
        back_ref[:, at] = nt(cot_ref[t], mix_ref[2]).astype(BF16)
    out_ref[:, :features] = nn(send_ref[...], hidden_ref[...]).astype(BF16)
    out_ref[:, features:] = tn(far_ref[...], back_ref[...]).astype(BF16)


def rows_of(index, width):
    return pl.ds(pl.multiple_of(index * width, 16), width)


def exchange(devices, out_ref, in_ref, send_sem, recv_sem):
    slots, lanes = out_ref.shape
    width = slots // devices
    half = lanes // 2
    me = lax.axis_index("dom")
    barrier = pltpu.get_barrier_semaphore()
    for d in range(1, devices):
        pl.semaphore_signal(
            barrier,
            inc=1,
            device_id={"dom": lax.rem(me + d, devices)},
            device_id_type=pl.DeviceIdType.MESH,
        )
    pl.semaphore_wait(barrier, devices - 1)
    groups = []
    for k, span in enumerate((slice(half, lanes), slice(0, half))):
        copies = []
        for d in range(1, devices):
            other = lax.rem(me + d, devices)
            copy = pltpu.make_async_remote_copy(
                src_ref=out_ref.at[rows_of(other, width), span],
                dst_ref=in_ref.at[rows_of(me, width), span],
                send_sem=send_sem.at[k, d - 1],
                recv_sem=recv_sem.at[k, d - 1],
                device_id={"dom": other},
                device_id_type=pl.DeviceIdType.MESH,
            )
            copy.start()
            copies.append(copy)
        groups.append(copies)
    in_ref[rows_of(me, width), :] = out_ref[rows_of(me, width), :]
    return groups


def mid_kernel(
    devices,
    own_ref,
    far_ref,
    send_ref,
    hidden_ref,
    back_ref,
    cot_ref,
    mix_ref,
    leave_ref,
    hop_ref,
    next_ref,
    out_ref,
    in_ref,
    hop_sum,
    next_sum,
    send_sem,
    recv_sem,
):
    features = hidden_ref.shape[1]
    chans = mix_ref.shape[1]
    spans = [slice(t * chans, (t + 1) * chans) for t in range(features // chans)]
    late, early = exchange(devices, leave_ref, in_ref, send_sem, recv_sem)
    for t, at in enumerate(spans):
        next_sum[:, at] = nt(cot_ref[t], mix_ref[1]) + tn(own_ref[...], back_ref[:, at])
        hop_sum[:, at] = nn(own_ref[...], hidden_ref[:, at])
    for copy in late:
        copy.wait_recv()
    next_ref[...] = (next_sum[...] + tn(send_ref[...], in_ref[:, features:])).astype(BF16)
    out_ref[:, features:] = tn(far_ref[...], next_ref[...]).astype(BF16)
    for copy in early:
        copy.wait_recv()
    hop_ref[...] = (hop_sum[...] + nn(far_ref[...], in_ref[:, :features])).astype(BF16)
    out_ref[:, :features] = nn(send_ref[...], hop_ref[...]).astype(BF16)
    for copy in late + early:
        copy.wait_send()


def post_kernel(
    devices,
    own_ref,
    far_ref,
    send_ref,
    hidden_ref,
    hop_ref,
    back_ref,
    leave_ref,
    sig_ref,
    cot_ref,
    tanh_ref,
    gate_ref,
    conv_ref,
    mix_ref,
    layer_ref,
    grad_ref,
    weight_ref,
    in_ref,
    hop_sum,
    layer_sum,
    hidden_sum,
    taps_ref,
    last_ref,
    held_ref,
    send_sem,
    recv_sem,
):
    features = hidden_ref.shape[1]
    chans = mix_ref.shape[1]
    spans = [slice(t * chans, (t + 1) * chans) for t in range(features // chans)]
    late, early = exchange(devices, leave_ref, in_ref, send_sem, recv_sem)

    def add_weight(spot, part, first):
        place = slice(spot * chans, (spot + 1) * chans)
        weight_ref[place, :] = part if first else weight_ref[place, :] + part

    fill_taps(conv_ref, taps_ref)
    for t, at in enumerate(spans):
        hidden_sum[:, at] = nt(cot_ref[t], mix_ref[0]) + tn(own_ref[...], back_ref[:, at])
        hop_sum[:, at] = nn(own_ref[...], hop_ref[:, at])
        layer_sum[:, at] = (
            sig_ref[:, (t + 1) * chans : (t + 2) * chans].astype(F32)
            + nn(hidden_ref[:, at], mix_ref[0])
            + nn(hop_ref[:, at], mix_ref[1])
        )
        add_weight(4, tn(hidden_ref[:, at], cot_ref[t]), t == 0)
        add_weight(5, tn(hop_ref[:, at], cot_ref[t]), t == 0)

    for copy in late:
        copy.wait_recv()
    for t, at in enumerate(spans):
        cot = cot_ref[t]
        grad_hidden = hidden_sum[:, at] + tn(
            send_ref[...], in_ref[:, features + t * chans : features + (t + 1) * chans]
        )
        tanh_filt = tanh_ref[:, at]
        sig_gate = gate_ref[:, at]
        held_ref[:, :chans] = (
            grad_hidden * sig_gate * (1.0 - tanh_filt * tanh_filt)
        ).astype(BF16)
        held_ref[:, chans:] = (grad_hidden * tanh_filt * sig_gate * (1.0 - sig_gate)).astype(BF16)
        outer = tn(sig_ref[:, t * chans : (t + 2) * chans], held_ref[...])
        for kind in range(2):
            for tap in range(2):
                part = outer[tap * chans : (tap + 1) * chans, kind * chans : (kind + 1) * chans]
                add_weight(kind * 2 + tap, part, t == 0)
        into = nt(held_ref[...], taps_ref[...])
        before = into[:, :chans]
        if t > 0:
            before = before + carried
        grad_ref[:, at] = before.astype(BF16)
        carried = into[:, chans:] + cot.astype(F32)
    grad_ref[:, features:] = carried.astype(BF16)

    for copy in early:
        copy.wait_recv()
    for t, at in enumerate(spans):
        last_ref[...] = (hop_sum[:, at] + nn(far_ref[...], in_ref[:, at])).astype(BF16)
        layer_ref[t] = (layer_sum[:, at] + nn(last_ref[...], mix_ref[2])).astype(BF16)
        add_weight(6, tn(last_ref[...], cot_ref[t]), t == 0)
    for copy in late + early:
        copy.wait_send()


def pairs_of(axis, size):
    stages, stride = [], 1
    while stride < size:
        stages.append((axis, stride, 2))
        stride *= 2
    return stages


def plan_of(order, rows):
    plan, count = [], rows
    for axis, stride, size in order:
        split = count % (size * 16) == 0
        if split:
            count //= size
        plan.append((axis, stride, size, split, count))
    return plan


def colours_of(axis_sizes, rows, chans):
    sizes = dict(axis_sizes)
    batch = pairs_of("batch", sizes["batch"])
    first, rest = batch[:1], batch[1:]
    direct = [("dom", 1, sizes["dom"])]
    pairs = pairs_of("dom", sizes["dom"])
    share = (rows // chans + 1) // 2 * chans
    for middle in (direct, pairs):
        colours = [
            (0, share, plan_of(first + rest + middle, share)),
            (share, rows - share, plan_of(first + middle + rest, rows - share)),
        ]
        if all(split or size == 2 for _, _, plan in colours for _, _, size, split, _ in plan):
            break
    return colours


def narrow(stage, split):
    return split and stage in (1, 2)


def landing_rows(colours, wanted):
    return sum(
        count * (size - 1)
        for _, _, plan in colours
        for stage, (_, _, size, split, count) in enumerate(plan)
        if narrow(stage, split) == wanted
    )


def others_of(axis, stride, size):
    index = lax.axis_index(axis)
    place = lax.rem(lax.div(index, stride), size)
    base = index - place * stride
    seats = [lax.rem(place + d, size) for d in range(1, size)]
    return place, [(seat, base + seat * stride) for seat in seats]


def reduce_kernel(
    colours,
    factor,
    grads_ref,
    out_ref,
    total,
    wide,
    landed,
    leaving,
    send_sem,
    recv_sem,
    back_send,
    back_recv,
):
    barrier = pltpu.get_barrier_semaphore()
    peers = sorted({(axis, stride, size) for axis, stride, size, _, _ in colours[0][2]})
    for axis, stride, size in peers:
        for _, other in others_of(axis, stride, size)[1]:
            pl.semaphore_signal(
                barrier, inc=1, device_id={axis: other}, device_id_type=pl.DeviceIdType.MESH
            )
    pl.semaphore_wait(barrier, sum(size - 1 for _, _, size in peers))

    starts = [base for base, _, _ in colours]
    trail = [[] for _ in colours]
    used = {True: 0, False: 0}
    depth = len(colours[0][2])
    for s in range(depth):
        moves = []
        for c, (_, _, plan) in enumerate(colours):
            axis, stride, size, split, count = plan[s]
            small = narrow(s, split)
            landing = landed if small else wide
            place, others = others_of(axis, stride, size)
            source = grads_ref if s == 0 else total
            keep = starts[c] + place * count if split else starts[c]
            keep_rows = pl.ds(pl.multiple_of(keep, 16), count)
            arrivals = []
            for d, (seat, other) in enumerate(others):
                give = starts[c] + seat * count if split else starts[c]
                give_rows = pl.ds(pl.multiple_of(give, 16), count)
                spot = pl.ds(used[small], count)
                if small:
                    leaving[spot, :] = source[give_rows, :].astype(BF16)
                copy = pltpu.make_async_remote_copy(
                    src_ref=leaving.at[spot] if small else source.at[give_rows],
                    dst_ref=landing.at[spot],
                    send_sem=send_sem.at[c, s, d],
                    recv_sem=recv_sem.at[c, s, d],
                    device_id={axis: other},
                    device_id_type=pl.DeviceIdType.MESH,
                )
                copy.start()
                arrivals.append((copy, spot))
                used[small] += count
            moves.append((arrivals, landing, source, keep_rows))
            trail[c].append(keep)
            starts[c] = keep
        for arrivals, landing, source, keep_rows in moves:
            for copy, _ in arrivals:
                copy.wait()
            value = source[keep_rows, :]
            for _, spot in arrivals:
                value = value + landing[spot, :].astype(F32)
            total[keep_rows, :] = value

    for c, (_, _, plan) in enumerate(colours):
        rows = pl.ds(pl.multiple_of(starts[c], 16), plan[-1][4])
        out_ref[rows, :] = (total[rows, :] * factor).astype(BF16)
    for s in range(depth - 1, -1, -1):
        moves = []
        for c, (_, _, plan) in enumerate(colours):
            axis, stride, size, split, count = plan[s]
            if not split:
                continue
            rows = pl.ds(pl.multiple_of(trail[c][s], 16), count)
            for d, (_, other) in enumerate(others_of(axis, stride, size)[1]):
                copy = pltpu.make_async_remote_copy(
                    src_ref=out_ref.at[rows],
                    dst_ref=out_ref.at[rows],
                    send_sem=back_send.at[c, s, d],
                    recv_sem=back_recv.at[c, s, d],
                    device_id={axis: other},
                    device_id_type=pl.DeviceIdType.MESH,
                )
                copy.start()
                moves.append(copy)
        for copy in moves:
            copy.wait()


def reduce_weights(grads, axis_sizes, factor, chans):
    rows, lanes = grads.shape
    colours = colours_of(axis_sizes, rows, chans)
    most = max(size for _, _, size, _, _ in colours[0][2]) - 1
    sems = pltpu.SemaphoreType.DMA((len(colours), len(colours[0][2]), most))
    slim = landing_rows(colours, True)
    return pl.pallas_call(
        functools.partial(reduce_kernel, colours, factor),
        out_shape=jax.ShapeDtypeStruct((rows, lanes), BF16),
        in_specs=[VMEM],
        out_specs=VMEM,
        scratch_shapes=[
            pltpu.VMEM((rows, lanes), F32),
            pltpu.VMEM((landing_rows(colours, False), lanes), F32),
            pltpu.VMEM((slim, lanes), BF16),
            pltpu.VMEM((slim, lanes), BF16),
            sems,
            sems,
            sems,
            sems,
        ],
        compiler_params=pltpu.CompilerParams(collective_id=0, has_side_effects=True),
        name="reduce_weights",
    )(grads)


def shape_of(*dims, dtype=BF16):
    return jax.ShapeDtypeStruct(dims, dtype)


def body(
    axis_sizes,
    signal,
    cotangent,
    conv_weight,
    mix_weight,
    send_rows,
    send_mask,
    tile_vals,
    tile_row,
    tile_col,
    tile_mask,
    hub_owner,
    hub_rows,
):
    nodes, b_dev, steps, chans = signal.shape
    out_steps = steps - 1
    features = out_steps * chans
    n_dom, cap = send_rows.shape
    hub_per = hub_rows.shape[1]
    width = -(-(cap + hub_per) // 16) * 16
    slots = n_dom * width
    block = tile_vals.shape[1]
    all_tiles = (nodes + n_dom * cap + hub_rows.size) // block

    sig = signal.reshape(nodes, steps * chans)
    cot = jnp.transpose(cotangent.reshape(nodes, out_steps, chans), (1, 0, 2))

    slot = np.arange(slots)
    expand = (slot[:, None] // width == np.arange(n_dom)[None, :]).astype(np.float32)
    lane = (slot % width).astype(np.int32)[:, None]
    entry = np.arange(n_dom * cap)
    halo = jnp.asarray(
        (entry // cap * width + entry % cap)[:, None] == slot[None, :], dtype=BF16
    )

    own, far, send, hidden, tanh_filt, sig_gate, back_two, out_one = pl.pallas_call(
        pre_kernel,
        out_shape=(
            shape_of(nodes, nodes),
            shape_of(nodes, slots),
            shape_of(slots, nodes),
            shape_of(nodes, features),
            shape_of(nodes, features, dtype=F32),
            shape_of(nodes, features, dtype=F32),
            shape_of(nodes, features),
            shape_of(slots, 2 * features),
        ),
        in_specs=[SMEM] * 3 + [VMEM] * 5 + [SMEM] + [VMEM] * 6,
        out_specs=(VMEM,) * 8,
        scratch_shapes=[
            pltpu.VMEM((all_tiles, nodes, block), F32),
            pltpu.VMEM((n_dom * cap + hub_rows.size, slots), BF16),
            pltpu.VMEM((2 * chans, 2 * chans), BF16),
        ],
        name="pre",
    )(
        tile_row,
        tile_col,
        tile_mask,
        sig,
        cot,
        conv_weight,
        mix_weight,
        tile_vals,
        hub_owner,
        send_rows,
        send_mask,
        hub_rows,
        expand,
        lane,
        halo,
    )

    sems = pltpu.SemaphoreType.DMA((2, n_dom - 1))
    landing = pltpu.VMEM((slots, 2 * features), BF16)
    partial = pltpu.VMEM((nodes, features), F32)
    hop_one, back_one, out_two = pl.pallas_call(
        functools.partial(mid_kernel, n_dom),
        out_shape=(
            shape_of(nodes, features),
            shape_of(nodes, features),
            shape_of(slots, 2 * features),
        ),
        in_specs=[VMEM] * 8,
        out_specs=(VMEM,) * 3,
        scratch_shapes=[landing, partial, partial, sems, sems],
        compiler_params=pltpu.CompilerParams(collective_id=1, has_side_effects=True),
        name="mid",
    )(own, far, send, hidden, back_two, cot, mix_weight, out_one)
    layer_out, signal_grad, grads = pl.pallas_call(
        functools.partial(post_kernel, n_dom),
        out_shape=(
            shape_of(out_steps, nodes, chans),
            shape_of(nodes, steps * chans),
            shape_of(7 * chans, chans, dtype=F32),
        ),
        in_specs=[VMEM] * 13,
        out_specs=(VMEM,) * 3,
        scratch_shapes=[
            landing,
            partial,
            partial,
            partial,
            pltpu.VMEM((2 * chans, 2 * chans), BF16),
            pltpu.VMEM((nodes, chans), BF16),
            pltpu.VMEM((nodes, 2 * chans), BF16),
            sems,
            sems,
        ],
        compiler_params=pltpu.CompilerParams(collective_id=2, has_side_effects=True),
        name="post",
    )(
        own,
        far,
        send,
        hidden,
        hop_one,
        back_one,
        out_two,
        sig,
        cot,
        tanh_filt,
        sig_gate,
        conv_weight,
        mix_weight,
    )
    total_count = nodes * out_steps * b_dev
    for _, size in axis_sizes:
        total_count *= size
    reduced = reduce_weights(grads, axis_sizes, 1.0 / math.sqrt(total_count), chans)
    return (
        jnp.transpose(layer_out, (1, 0, 2)).reshape(nodes, b_dev, out_steps, chans),
        signal_grad.reshape(signal.shape),
        reduced[: 4 * chans].astype(F32).reshape(conv_weight.shape),
        reduced[4 * chans :].astype(F32).reshape(mix_weight.shape),
    )


def solution(mesh):
    placed = (
        P("dom", "batch", None, None),
        P("dom", "batch", None, None),
        P(),
        P(),
        P("dom", None),
        P("dom", None),
        P("dom", None, None),
        P("dom"),
        P("dom"),
        P("dom"),
        P(),
        P(),
    )
    axis_sizes = tuple((axis, mesh.shape[axis]) for axis in ("dom", "batch"))
    return jax.shard_map(
        functools.partial(body, axis_sizes),
        mesh=mesh,
        in_specs=placed,
        out_specs=(P("dom", "batch", None, None), P("dom", "batch", None, None), P(), P()),
        check_vma=False,
    )
```
